32 devices in a mesh: expert: 16 (over z, y, core), hidden: 2 (over x).
Axes of the slice: x: 2, y: 2, z: 4, core: 2. Of those that a mesh axis runs over, the one named last changes fastest.
Arguments:
- tokens: bfloat16 [2048, 4096], P('expert'), may hold values from -6 to 6
- enc_weight: bfloat16 [4096, 1024], P('expert', 'hidden'), may hold values from -0.09375 to 0.09375
- routes: int32 [2048, 8], P('expert'), may hold values from 0 to 15, all different within a row; in each aligned block of 128 rows (0 to 127, 128 to 255, ...) at most 128 rows name the same one
- gates: float32 [2048, 8], P('expert'), may hold values from 0.1 to 1
- gate_weight: bfloat16 [16, 1024, 1536], P('expert', None, 'hidden'), may hold values from -0.1875 to 0.1875
- up_weight: bfloat16 [16, 1024, 1536], P('expert', None, 'hidden'), may hold values from -0.1875 to 0.1875
- down_weight: bfloat16 [16, 1536, 1024], P('expert', None, 'hidden'), may hold values from -0.15625 to 0.15625
- dec_weight: bfloat16 [1024, 4096], P('expert', 'hidden'), may hold values from -0.1875 to 0.1875
Outputs:
- mixed: bfloat16 [2048, 4096], P('expert', 'hidden')
The draws below stay inside these ranges and needn't reach their ends.
Inputs may be any that keep to these rules, and one draw needn't show every extreme that they name: `routes`: each row names 8 different experts; within one group of 128 consecutive tokens no expert is named more than 128 times.
All inputs are finite; a program needn't handle non-finite values.
Results may differ from the reference program's by a relative error of at most 0.0076.
Values may be sent and summed in bfloat16 or wider, within the bound.
A program may use at most 64 MiB of HBM per device.

```python
import math
import jax
import jax.numpy as jnp
import numpy as np
from jax import lax

D = 4096
LATENT = 1024
FF = 1536
TOP = 8
TOK_DEV = 128
EXPERTS = 16
TOKENS = 2048
CAP = 128
N_EXPERT = 16


def steps_of(rng, shape, split, smallest, largest):
    gain = 1.0
    for axis_at, parts in split:
        heights = jax.random.uniform(jax.random.fold_in(jax.random.fold_in(rng, 6), axis_at), (parts,), jnp.float32, smallest / len(split), largest / len(split))
        gain = gain * jnp.repeat(jnp.exp(heights), shape[axis_at] // parts).reshape((-1,) + (1,) * (len(shape) - 1 - axis_at))
    return gain


def assign_block(stream_key, own, number, rows, number_of, top, reach, slope):
    ranking = jax.random.permutation(stream_key, number_of)
    crowded, ordinary = portions_of(number_of, rows * top, reach, slope, True), portions_of(number_of, rows * top, reach, slope, False)
    places = jnp.arange(number_of)

    def named(lengths, turn):
        used = int((lengths > 0).sum())
        fixed = max(1, used // 4)
        moved = fixed + (places - fixed + turn * (used - fixed)) % max(1, number_of - fixed)
        return jnp.zeros((number_of,), jnp.int32).at[ranking[jnp.where(places < fixed, places, moved)]].set(jnp.asarray(lengths, jnp.int32))

    lengths = jnp.where(number % 4 == 0, named(crowded, number // 4), named(ordinary, number - number // 4 - 1))
    mixed = jax.random.permutation(jax.random.fold_in(own, 3), number_of)
    source_of, sink = mixed[0:number_of // 2 * 2:2], mixed[1:number_of // 2 * 2:2]
    room = jnp.minimum(lengths[source_of] - 1, reach - lengths[sink]) // 2
    room = jnp.where((source_of == ranking[0]) | (sink == ranking[0]) | (lengths[sink] == 0), 0, jnp.maximum(room, 0))
    moved = jax.random.randint(jax.random.fold_in(own, 4), (number_of // 2,), 0, 1 << 20) % (room + 1)
    lengths = lengths.at[source_of].add(-moved).at[sink].add(moved)
    items = jnp.searchsorted(jnp.cumsum(lengths), jnp.arange(rows * top), side="right").astype(jnp.int32)
    listing = items.reshape(top, rows).T
    listing = listing[jax.random.permutation(jax.random.fold_in(own, 1), rows)]
    turn = jax.random.randint(jax.random.fold_in(own, 2), (rows, 1), 0, top)
    return jnp.take_along_axis(listing, (jnp.arange(top)[None, :] + turn) % top, axis=1)


def portions_of(count, total, limit, skew, full):
    portions = [(1 << 20) // math.isqrt(grade ** skew) + 1 for grade in range(1, count + 1)]
    largest = limit if full else min(limit, max(-(-total // count), total * portions[0] // sum(portions)))
    least = 1 if total - largest >= count - 1 else 0
    counts, spare = [largest] + [least] * (count - 1), total - largest - least * (count - 1)
    while spare > 0:
        movable = [i for i in range(1, count) if counts[i] < largest] or [i for i in range(1, count) if counts[i] < limit]
        pool, budget = sum([portions[i] for i in movable]), spare
        for i in movable:
            addition = min(limit - counts[i], max(1, budget * portions[i] // pool), spare)
            counts[i] = counts[i] + addition
            spare = spare - addition
    return np.array(counts)


def normal_values(own_key, dims, deviation, limit, cuts=(), kind=jnp.bfloat16):
    loudness = steps_of(own_key, dims, cuts, -0.22, 0.18) if cuts else 1.0
    drawn = jax.random.normal(own_key, dims, jnp.float32) * deviation * loudness
    return jnp.minimum(jnp.maximum(drawn, -limit), limit).astype(kind)


def setup_inputs(seed: int = 0) -> dict:
    streams_of = jax.random.split(jax.random.key(seed), 9)
    tokens = normal_values(streams_of[0], (TOKENS, D), 1.0, 6.0, ((0, 16),))
    enc_weight = normal_values(streams_of[1], (D, LATENT), D ** -0.5, 0.09375, ((0, 16), (1, 2)))
    routes_keys = jax.random.split(jax.random.fold_in(streams_of[2], 1), TOKENS // TOK_DEV)
    routes_turns = jax.random.permutation(jax.random.fold_in(streams_of[2], 3), TOKENS // TOK_DEV)
    routes = jax.vmap(lambda own, number: assign_block(jax.random.fold_in(streams_of[2], 2), own, number, TOK_DEV, EXPERTS, TOP, CAP, 2))(routes_keys, routes_turns).reshape((TOKENS, TOP))
    gates = jnp.clip(0.1 + 0.9 * jax.random.uniform(streams_of[3], (TOKENS, TOP), jnp.float32) ** steps_of(streams_of[3], (TOKENS, TOP), ((0, 16),), -0.2, 0.2), 0.1, 1.0)
    gate_weight = normal_values(streams_of[4], (EXPERTS, LATENT, FF), LATENT ** -0.5, 0.1875, ((0, 16), (2, 2)))
    up_weight = normal_values(streams_of[5], (EXPERTS, LATENT, FF), LATENT ** -0.5, 0.1875, ((0, 16), (2, 2)))
    down_weight = normal_values(streams_of[6], (EXPERTS, FF, LATENT), FF ** -0.5, 0.15625, ((0, 16), (2, 2)))
    dec_weight = normal_values(streams_of[7], (LATENT, D), LATENT ** -0.5, 0.1875, ((0, 16), (1, 2)))
    return {"tokens": tokens, "enc_weight": enc_weight, "routes": routes, "gates": gates, "gate_weight": gate_weight, "up_weight": up_weight, "down_weight": down_weight, "dec_weight": dec_weight}


def reference(tokens, enc_weight, routes, gates, gate_weight, up_weight, down_weight, dec_weight):
    latent = jnp.dot(tokens, enc_weight, preferred_element_type=jnp.float32).astype(jnp.bfloat16)
    group_count = TOKENS // TOK_DEV
    blocked = routes.reshape(group_count, TOK_DEV * TOP)

    def ranks(chosen):
        onehot = (chosen[:, None] == jnp.arange(EXPERTS, dtype=jnp.int32)[None, :]).astype(jnp.int32)
        earlier = jnp.cumsum(onehot, axis=0) - onehot
        return jnp.sum(earlier * onehot, axis=1).astype(jnp.int32)

    position = lax.map(ranks, blocked)
    group_ids = jnp.arange(group_count, dtype=jnp.int32)[:, None]
    slot_rows = N_EXPERT * CAP
    target = (blocked * slot_rows + group_ids * CAP + position).reshape(-1).astype(jnp.int32)
    source_row = (jnp.arange(TOKENS * TOP, dtype=jnp.int32) // TOP).astype(jnp.int32)
    slots = jnp.zeros((EXPERTS * slot_rows, LATENT), jnp.bfloat16).at[target].set(latent[source_row])
    slots = slots.reshape(EXPERTS, slot_rows, LATENT)

    def expert(inputs):
        arrived, gate_matrix, up_matrix, down_matrix = inputs
        gate_part = jnp.dot(arrived, gate_matrix, preferred_element_type=jnp.float32)
        up_part = jnp.dot(arrived, up_matrix, preferred_element_type=jnp.float32)
        activation = (jax.nn.silu(gate_part) * up_part).astype(jnp.bfloat16)
        return jnp.dot(activation, down_matrix, preferred_element_type=jnp.float32).astype(jnp.bfloat16)

    answer = lax.map(expert, (slots, gate_weight, up_weight, down_weight)).reshape(EXPERTS * slot_rows, LATENT)
    picked = answer[target].astype(jnp.float32).reshape(TOKENS, TOP, LATENT)
    combined = jnp.sum(picked * gates[:, :, None], axis=1).astype(jnp.bfloat16)
    return jnp.dot(combined, dec_weight, preferred_element_type=jnp.float32).astype(jnp.bfloat16)
```

```python
import jax
import jax.numpy as jnp
from jax import lax
from jax.sharding import PartitionSpec as P


def exchange_slots(tokens, enc_weight, routes, gates, gate_weight, up_weight, down_weight, dec_weight):
    groups = lax.axis_size("expert")
    token_count, choice_count = routes.shape
    capacity = min(token_count, 2 * token_count * choice_count // groups)
    columns = tokens
    latent = jnp.dot(
        columns,
        lax.all_gather(enc_weight, "expert", axis=0, tiled=True),
        preferred_element_type=jnp.float32,
    ).astype(jnp.bfloat16)
    payload = lax.all_gather(latent, "hidden", axis=1, tiled=True)
    chosen = routes.reshape(-1)
    onehot = (chosen[:, None] == jnp.arange(groups, dtype=jnp.int32)[None, :]).astype(jnp.int32)
    position = jnp.sum((jnp.cumsum(onehot, axis=0) - onehot) * onehot, axis=1)
    target = chosen * capacity + position
    source_row = jnp.arange(token_count * choice_count, dtype=jnp.int32) // choice_count
    payload_width = payload.shape[1]
    outgoing = (
        jnp.zeros((groups * capacity, payload_width), jnp.bfloat16)
        .at[target]
        .set(payload[source_row])
    )
    outgoing = outgoing.reshape(groups, capacity, payload_width)
    gate_matrix = gate_weight[0]
    up_matrix = up_weight[0]
    down_matrix = down_weight[0]
    arrived = lax.all_to_all(outgoing, "expert", split_axis=0, concat_axis=0, tiled=True)
    slot_count = arrived.shape[1]
    inputs = arrived.reshape(groups * slot_count, arrived.shape[2])
    gate_part = jnp.dot(inputs, gate_matrix, preferred_element_type=jnp.float32)
    up_part = jnp.dot(inputs, up_matrix, preferred_element_type=jnp.float32)
    activation = (jax.nn.silu(gate_part) * up_part).astype(jnp.bfloat16)
    answer = jnp.dot(
        lax.all_gather(activation, "hidden", axis=1, tiled=True),
        down_matrix,
        preferred_element_type=jnp.float32,
    ).astype(jnp.bfloat16)
    answer = answer.reshape(groups, slot_count, down_matrix.shape[1])
    returned_rows = lax.all_to_all(answer, "expert", split_axis=0, concat_axis=0, tiled=True)
    returned_rows = returned_rows.reshape(groups * capacity, returned_rows.shape[2])
    picked = returned_rows[target].astype(jnp.float32).reshape(token_count, choice_count, -1)
    combined = jnp.sum(picked * gates[:, :, None], axis=1).astype(jnp.bfloat16)
    combined_all = lax.all_gather(combined, "hidden", axis=1, tiled=True)
    columns = combined_all
    return jnp.dot(
        columns,
        lax.all_gather(dec_weight, "expert", axis=0, tiled=True),
        preferred_element_type=jnp.float32,
    ).astype(jnp.bfloat16)


def every_token(tokens, enc_weight, routes, gates, gate_weight, up_weight, down_weight, dec_weight):
    groups = lax.axis_size("expert")
    latent = jnp.dot(
        tokens,
        lax.all_gather(enc_weight, "expert", axis=0, tiled=True),
        preferred_element_type=jnp.float32,
    ).astype(jnp.bfloat16)
    payload = lax.all_gather(latent, "hidden", axis=1, tiled=True)
    inputs = lax.all_gather(payload, "expert", axis=0, tiled=True)
    onehot = routes[:, :, None] == jnp.arange(groups, dtype=jnp.int32)[None, None, :]
    shares = jnp.sum(jnp.where(onehot, gates[:, :, None], 0.0), axis=1)
    shares = lax.all_to_all(shares.T, "expert", split_axis=0, concat_axis=1, tiled=True)
    down = lax.all_to_all(down_weight[0], "hidden", split_axis=0, concat_axis=1, tiled=True)
    gate_part = jnp.dot(inputs, gate_weight[0], preferred_element_type=jnp.float32)
    up_part = jnp.dot(inputs, up_weight[0], preferred_element_type=jnp.float32)
    activation = (jax.nn.silu(gate_part) * up_part).astype(jnp.bfloat16)
    answer = jnp.dot(activation, down, preferred_element_type=jnp.float32)
    answer = (answer * shares.reshape(-1)[:, None]).astype(jnp.bfloat16)
    combined = lax.psum_scatter(answer, "expert", scatter_dimension=0, tiled=True)
    combined = lax.psum(combined, "hidden")
    return jnp.dot(
        combined,
        lax.all_gather(dec_weight, "expert", axis=0, tiled=True),
        preferred_element_type=jnp.float32,
    ).astype(jnp.bfloat16)


def on_device(tokens, enc_weight, routes, *rest):
    token_count, choice_count = routes.shape
    plan = every_token if 2 * choice_count >= lax.axis_size("expert") else exchange_slots
    return plan(tokens, enc_weight, routes, *rest)


def solution(mesh):
    in_specs = (
        P("expert", None),
        P("expert", "hidden"),
        P("expert", None),
        P("expert", None),
        P("expert", None, "hidden"),
        P("expert", None, "hidden"),
        P("expert", None, "hidden"),
        P("expert", "hidden"),
    )
    out_specs = P("expert", "hidden")
    return jax.shard_map(
        on_device, mesh=mesh, in_specs=in_specs, out_specs=out_specs, check_vma=False
    )
```

```python
import jax
import jax.numpy as jnp
from jax import lax
from jax.experimental import pallas as pl
from jax.experimental.pallas import tpu as pltpu
from jax.sharding import PartitionSpec as P


def exchange_slots(tokens, enc_weight, routes, gates, gate_weight, up_weight, down_weight, dec_weight):
    groups = lax.axis_size("expert")
    token_count, choice_count = routes.shape
    capacity = min(token_count, 2 * token_count * choice_count // groups)
    columns = tokens
    latent = jnp.dot(
        columns,
        lax.all_gather(enc_weight, "expert", axis=0, tiled=True),
        preferred_element_type=jnp.float32,
    ).astype(jnp.bfloat16)
    payload = lax.all_gather(latent, "hidden", axis=1, tiled=True)
    chosen = routes.reshape(-1)
    onehot = (chosen[:, None] == jnp.arange(groups, dtype=jnp.int32)[None, :]).astype(jnp.int32)
    position = jnp.sum((jnp.cumsum(onehot, axis=0) - onehot) * onehot, axis=1)
    target = chosen * capacity + position
    source_row = jnp.arange(token_count * choice_count, dtype=jnp.int32) // choice_count
    payload_width = payload.shape[1]
    outgoing = (
        jnp.zeros((groups * capacity, payload_width), jnp.bfloat16)
        .at[target]
        .set(payload[source_row])
    )
    outgoing = outgoing.reshape(groups, capacity, payload_width)
    gate_matrix = gate_weight[0]
    up_matrix = up_weight[0]
    down_matrix = down_weight[0]
    arrived = lax.all_to_all(outgoing, "expert", split_axis=0, concat_axis=0, tiled=True)
    slot_count = arrived.shape[1]
    inputs = arrived.reshape(groups * slot_count, arrived.shape[2])
    gate_part = jnp.dot(inputs, gate_matrix, preferred_element_type=jnp.float32)
    up_part = jnp.dot(inputs, up_matrix, preferred_element_type=jnp.float32)
    activation = (jax.nn.silu(gate_part) * up_part).astype(jnp.bfloat16)
    answer = jnp.dot(
        lax.all_gather(activation, "hidden", axis=1, tiled=True),
        down_matrix,
        preferred_element_type=jnp.float32,
    ).astype(jnp.bfloat16)
    answer = answer.reshape(groups, slot_count, down_matrix.shape[1])
    returned_rows = lax.all_to_all(answer, "expert", split_axis=0, concat_axis=0, tiled=True)
    returned_rows = returned_rows.reshape(groups * capacity, returned_rows.shape[2])
    picked = returned_rows[target].astype(jnp.float32).reshape(token_count, choice_count, -1)
    combined = jnp.sum(picked * gates[:, :, None], axis=1).astype(jnp.bfloat16)
    combined_all = lax.all_gather(combined, "hidden", axis=1, tiled=True)
    columns = combined_all
    return jnp.dot(
        columns,
        lax.all_gather(dec_weight, "expert", axis=0, tiled=True),
        preferred_element_type=jnp.float32,
    ).astype(jnp.bfloat16)


CORES, LINES = 2, 2
MESH = pl.DeviceIdType.MESH


def layer_kernel(
    tokens_hbm, enc, gate_hbm, up_hbm, down_hbm, dec, out,
    tokens, gate, up, down, enc_all, dec_all, latents, shares, activation,
    answers, core_in, x_out, x_in, keep, y_out, y_in, z_out, z_in, combined,
    enc_recv, enc_send, lat_recv, lat_send, dec_recv, dec_send,
    down_recv, down_send, core_recv, core_send, x_recv, x_send, y_recv, y_send,
    z_recv, z_send, last_recv, last_send, local_sem,
):
    groups = lax.axis_size("expert")
    depth = groups // (CORES * LINES)
    e = lax.axis_index("expert")
    h = lax.axis_index("hidden")
    c, y, z = e % CORES, (e // CORES) % LINES, e // (CORES * LINES)

    def at(zz, yy, cc):
        return (zz * LINES + yy) * CORES + cc

    def behind(s):
        return (z + depth - s) % depth

    rows = tokens.shape[0]
    half = latents.shape[2]
    enc_rows = tokens.shape[1] // groups
    band = LINES * CORES * rows
    y_peer = (at(z, 1 - y, c), h)
    core_peer = (at(z, y, 1 - c), h)
    x_peer = (e, 1 - h)
    z_peers = [(at((z + s) % depth, y, c), h) for s in range(1, depth)]

    waiting = []

    def send(src, dst, ssem, rsem, peer):
        copy = pltpu.make_async_remote_copy(
            src_ref=src, dst_ref=dst, send_sem=ssem, recv_sem=rsem,
            device_id=peer, device_id_type=MESH,
        )
        copy.start()
        waiting.append(copy)

    def arrive(dst, rsem):
        pltpu.make_async_copy(dst, dst, rsem).wait()

    barrier = pltpu.get_barrier_semaphore()
    peers = z_peers + [y_peer, core_peer, x_peer]
    for peer in peers:
        pl.semaphore_signal(barrier, inc=1, device_id=peer, device_id_type=MESH)
    pl.semaphore_wait(barrier, len(peers))

    class Gather:
        def __init__(self, own, buffer, rsem, ssem):
            self.own, self.buffer, self.rsem, self.ssem = own, buffer, rsem, ssem

        def forward(self, o, peer, slot, own=False):
            src = self.own if own else self.buffer.at[o]
            send(src, self.buffer.at[o], self.ssem.at[slot], self.rsem.at[o], peer)

        def wait(self, o):
            arrive(self.buffer.at[o], self.rsem.at[o])

        def start(self):
            for s in range(1, depth):
                self.forward(e, z_peers[s - 1], s - 1, True)
            self.forward(e, y_peer, depth - 1, True)
            self.forward(e, core_peer, 2 * depth - 1, True)

        def from_z(self, s):
            o = at(behind(s), y, c)
            self.wait(o)
            self.forward(o, y_peer, depth - 1 + s)
            self.forward(o, core_peer, 2 * depth - 1 + s)
            return o

        def from_y(self, s):
            o = at(behind(s), 1 - y, c)
            self.wait(o)
            self.forward(o, core_peer, 3 * depth - 1 + s)
            return o

        def from_core(self, s, yy):
            o = at(behind(s), yy, 1 - c)
            self.wait(o)
            return o

    enc_gather = Gather(enc, enc_all, enc_recv, enc_send)
    dec_gather = Gather(dec, dec_all, dec_recv, dec_send)
    enc_gather.start()

    local = [
        pltpu.make_async_copy(tokens_hbm, tokens, local_sem.at[0]),
        pltpu.make_async_copy(gate_hbm.at[0], gate, local_sem.at[1]),
        pltpu.make_async_copy(up_hbm.at[0], up, local_sem.at[2]),
    ]
    for copy in local:
        copy.start()
    part = down.shape[1]
    own_down = pltpu.make_async_copy(
        down_hbm.at[0, pl.ds(pl.multiple_of(h * part, part), part)], down.at[h], local_sem.at[3]
    )
    own_down.start()
    send(
        down_hbm.at[0, pl.ds(pl.multiple_of((1 - h) * part, part), part)],
        down.at[h], down_send.at[0], down_recv.at[0], x_peer,
    )

    local[0].wait()

    def enc_dot(o, block):
        columns = pl.ds(pl.multiple_of(o * enc_rows, enc_rows), enc_rows)
        return jnp.dot(tokens[:, columns], block[:enc_rows], preferred_element_type=jnp.float32)

    def take_shares(o, block):
        pieces = half // 128
        piece = rows // pieces
        for q in range(pieces):
            tile = block[enc_rows:, q * 128 : (q + 1) * 128].astype(jnp.float32)
            lane = lax.broadcasted_iota(jnp.int32, tile.shape, 1)
            mine = jnp.logical_and(lane % groups == e, lane < 3 * groups)
            total = jnp.sum(jnp.where(mine, tile, 0.0), axis=1, keepdims=True)
            start = pl.multiple_of(o * rows + q * piece, piece)
            shares[pl.ds(start, piece), :] = jnp.broadcast_to(total, (piece, 128))

    total = enc_dot(e, enc[...])
    take_shares(e, enc[...])

    def landed(o, total):
        take_shares(o, enc_all[o])
        return total + enc_dot(o, enc_all[o])

    for s in range(1, depth + 1):
        if s < depth:
            total = landed(enc_gather.from_z(s), total)
        total = landed(enc_gather.from_y(s - 1), total)
    for s in range(depth):
        total = landed(enc_gather.from_core(s, y), total)
    for s in range(depth):
        total = landed(enc_gather.from_core(s, 1 - y), total)

    def lat(hh, o):
        return latents.at[hh, pl.ds(pl.multiple_of(o * rows, rows), rows)]

    def lat_forward(hh, o, peer, slot):
        send(lat(hh, o), lat(hh, o), lat_send.at[slot], lat_recv.at[hh, o], peer)

    def lat_wait(hh, o):
        arrive(lat(hh, o), lat_recv.at[hh, o])

    latents[h, pl.ds(pl.multiple_of(e * rows, rows), rows), :] = total.astype(jnp.bfloat16)
    base_y, base_x, base_c = depth, 2 * depth, 4 * depth
    for s in range(1, depth):
        lat_forward(h, e, z_peers[s - 1], s - 1)
    lat_forward(h, e, y_peer, base_y)
    lat_forward(h, e, x_peer, base_x)
    lat_forward(h, e, core_peer, base_c)

    def lat_z(s):
        o = at(behind(s), y, c)
        lat_wait(h, o)
        lat_forward(h, o, y_peer, base_y + s)
        lat_forward(h, o, x_peer, base_x + s)
        lat_forward(h, o, core_peer, base_c + s)

    def lat_y(s):
        o = at(behind(s), 1 - y, c)
        lat_wait(h, o)
        lat_forward(h, o, x_peer, base_x + depth + s)
        lat_forward(h, o, core_peer, base_c + depth + s)

    def lat_x(s):
        for k, yy in enumerate((y, 1 - y)):
            o = at(behind(s), yy, c)
            lat_wait(1 - h, o)
            lat_forward(1 - h, o, core_peer, base_c + (2 + k) * depth + s)

    def lat_core(s):
        for hh in (h, 1 - h):
            for yy in (y, 1 - y):
                lat_wait(hh, at(behind(s), yy, 1 - c))

    tile = 256

    def experts(s):
        start = pl.multiple_of(behind(s) * band, band)

        @pl.loop(0, gate.shape[1] // tile)
        def _(n):
            columns = pl.ds(pl.multiple_of(n * tile, tile), tile)
            low, high = latents[0, pl.ds(start, band), :], latents[1, pl.ds(start, band), :]
            g = jnp.dot(low, gate[:half, columns], preferred_element_type=jnp.float32)
            g += jnp.dot(high, gate[half:, columns], preferred_element_type=jnp.float32)
            u = jnp.dot(low, up[:half, columns], preferred_element_type=jnp.float32)
            u += jnp.dot(high, up[half:, columns], preferred_element_type=jnp.float32)
            activation[:, columns] = (g / (1.0 + jnp.exp(-g)) * u).astype(jnp.bfloat16)

        for hh in range(2):
            @pl.loop(0, half // tile)
            def _(n):
                columns = pl.ds(pl.multiple_of(n * tile, tile), tile)
                a = jnp.dot(activation[...], down[hh, :, columns], preferred_element_type=jnp.float32)
                a = (a * shares[pl.ds(start, band), 0:1]).astype(jnp.bfloat16)
                for b in range(LINES * CORES):
                    answers[s, b, hh, :, columns] = a[b * rows : (b + 1) * rows]

        for yy in range(LINES):
            send(
                answers.at[s, yy * CORES + 1 - c], core_in.at[s, yy],
                core_send.at[s, yy], core_recv.at[s, yy], core_peer,
            )

    def sum_cores(s):
        for yy in range(LINES):
            arrive(core_in.at[s, yy], core_recv.at[s, yy])
            mine = yy * CORES + c
            other = answers[s, mine, 1 - h].astype(jnp.float32)
            x_out[s, yy] = (other + core_in[s, yy, 1 - h].astype(jnp.float32)).astype(jnp.bfloat16)
        send(x_out.at[s], x_in.at[s], x_send.at[s], x_recv.at[s], x_peer)
        for yy in range(LINES):
            mine = yy * CORES + c
            keep[s, yy] = answers[s, mine, h].astype(jnp.float32) + core_in[s, yy, h].astype(jnp.float32)

    def sum_x(s):
        arrive(x_in.at[s], x_recv.at[s])
        y_out[s] = (keep[s, 1 - y] + x_in[s, 1 - y].astype(jnp.float32)).astype(jnp.bfloat16)
        send(y_out.at[s], y_in.at[s], y_send.at[s], y_recv.at[s], y_peer)
        keep[s, y] = keep[s, y] + x_in[s, y].astype(jnp.float32)

    def sum_y(s):
        arrive(y_in.at[s], y_recv.at[s])
        total = keep[s, y] + y_in[s].astype(jnp.float32)
        if s == 0:
            keep[s, y] = total
        else:
            z_out[s] = total.astype(jnp.bfloat16)
            peer = (at(behind(s), y, c), h)
            send(z_out.at[s], z_in.at[s], z_send.at[s], z_recv.at[s], peer)

    for s in range(1, depth + 1):
        if s < depth:
            lat_z(s)
        lat_y(s - 1)
    dec_gather.start()
    local[1].wait()
    local[2].wait()
    own_down.wait()
    arrive(down.at[1 - h], down_recv.at[0])
    for s in range(depth):
        lat_x(s)
        lat_core(s)
        experts(s)
        if s >= 1:
            sum_cores(s - 1)
        if s >= 2:
            sum_x(s - 2)
        if s >= 3:
            sum_y(s - 3)
        if s == 0:
            for k in range(1, depth):
                dec_gather.from_z(k)
        if s == 1:
            for k in range(depth):
                dec_gather.from_y(k)
    for s in range(depth, depth + 3):
        if s - 1 < depth:
            sum_cores(s - 1)
        if 0 <= s - 2 < depth:
            sum_x(s - 2)
        if 0 <= s - 3 < depth:
            sum_y(s - 3)
    final = keep[0, y]
    for s in range(1, depth):
        arrive(z_in.at[s], z_recv.at[s])
        final += z_in[s].astype(jnp.float32)
    combined[h] = final.astype(jnp.bfloat16)
    send(combined.at[h], combined.at[h], last_send.at[0], last_recv.at[0], x_peer)
    for s in range(depth):
        for yy in (y, 1 - y):
            dec_gather.from_core(s, yy)
    dec_all[e] = dec[...]
    arrive(combined.at[1 - h], last_recv.at[0])

    per = groups // 2

    @pl.loop(0, out.shape[1] // tile)
    def _(n):
        columns = pl.ds(pl.multiple_of(n * tile, tile), tile)
        low = dec_all[:per, :, columns].reshape(half, tile)
        high = dec_all[per:, :, columns].reshape(half, tile)
        m = jnp.dot(combined[0], low, preferred_element_type=jnp.float32)
        m += jnp.dot(combined[1], high, preferred_element_type=jnp.float32)
        out[:, columns] = m.astype(jnp.bfloat16)

    for copy in waiting:
        copy.wait_send()


def whole_layer(tokens, enc_weight, routes, gates, gate_weight, up_weight, down_weight, dec_weight):
    groups = lax.axis_size("expert")
    depth = groups // (CORES * LINES)
    rows, width = tokens.shape
    enc_rows, half = enc_weight.shape
    hidden = gate_weight.shape[2]
    onehot = routes[:, :, None] == jnp.arange(groups, dtype=jnp.int32)[None, None, :]
    rest = jnp.sum(jnp.where(onehot, gates[:, :, None], 0.0), axis=1)
    parts = []
    for _ in range(3):
        piece = lax.reduce_precision(rest, 8, 7)
        parts.append(piece.astype(jnp.bfloat16))
        rest = rest - piece
    packed = jnp.concatenate(parts, axis=1)
    packed = jnp.pad(packed, ((0, 0), (0, 128 - packed.shape[1])))
    pieces = half // 128
    packed = packed.reshape(pieces, rows // pieces, 128).transpose(1, 0, 2).reshape(-1, half)
    enc = jnp.concatenate([enc_weight, packed], axis=0)
    bf, f32 = jnp.bfloat16, jnp.float32
    band = LINES * CORES
    anywhere = pl.BlockSpec(memory_space=pl.ANY)
    vmem = pl.BlockSpec(memory_space=pltpu.VMEM)
    dma = pltpu.SemaphoreType.DMA
    scratch = [
        pltpu.VMEM((rows, width), bf),
        pltpu.VMEM(gate_weight.shape[1:], bf),
        pltpu.VMEM(up_weight.shape[1:], bf),
        pltpu.VMEM((2, hidden, half), bf),
        pltpu.VMEM((groups, *enc.shape), bf),
        pltpu.VMEM((groups, *dec_weight.shape), bf),
        pltpu.VMEM((2, groups * rows, half), bf),
        pltpu.VMEM((groups * rows, 128), f32),
        pltpu.VMEM((band * rows, hidden), bf),
        pltpu.VMEM((depth, band, 2, rows, half), bf),
        pltpu.VMEM((depth, LINES, 2, rows, half), bf),
        pltpu.VMEM((depth, LINES, rows, half), bf),
        pltpu.VMEM((depth, LINES, rows, half), bf),
        pltpu.VMEM((depth, LINES, rows, half), f32),
        pltpu.VMEM((depth, rows, half), bf),
        pltpu.VMEM((depth, rows, half), bf),
        pltpu.VMEM((depth, rows, half), bf),
        pltpu.VMEM((depth, rows, half), bf),
        pltpu.VMEM((2, rows, half), bf),
        dma((groups,)), dma((4 * depth,)),
        dma((2, groups)), dma((8 * depth,)),
        dma((groups,)), dma((4 * depth,)),
        dma((1,)), dma((1,)),
        dma((depth, LINES)), dma((depth, LINES)),
        dma((depth,)), dma((depth,)), dma((depth,)), dma((depth,)), dma((depth,)), dma((depth,)),
        dma((1,)), dma((1,)), dma((4,)),
    ]
    return pl.pallas_call(
        layer_kernel,
        out_shape=jax.ShapeDtypeStruct((rows, dec_weight.shape[1]), bf),
        in_specs=[anywhere, vmem, anywhere, anywhere, anywhere, vmem],
        out_specs=vmem,
        scratch_shapes=scratch,
        compiler_params=pltpu.CompilerParams(
            collective_id=0, has_side_effects=True, vmem_limit_bytes=60 * 1024 * 1024
        ),
    )(tokens, enc, gate_weight, up_weight, down_weight, dec_weight)


def on_device(tokens, enc_weight, routes, *rest):
    token_count, choice_count = routes.shape
    plan = whole_layer if 2 * choice_count >= lax.axis_size("expert") else exchange_slots
    return plan(tokens, enc_weight, routes, *rest)


def solution(mesh):
    in_specs = (
        P("expert", None),
        P("expert", "hidden"),
        P("expert", None),
        P("expert", None),
        P("expert", None, "hidden"),
        P("expert", None, "hidden"),
        P("expert", None, "hidden"),
        P("expert", "hidden"),
    )
    out_specs = P("expert", "hidden")
    return jax.shard_map(
        on_device, mesh=mesh, in_specs=in_specs, out_specs=out_specs, check_vma=False
    )
```

```python
import jax
import jax.numpy as jnp
from jax import lax
from jax.experimental import pallas as pl
from jax.experimental.pallas import tpu as pltpu
from jax.sharding import PartitionSpec as P


def exchange_slots(tokens, enc_weight, routes, gates, gate_weight, up_weight, down_weight, dec_weight):
    groups = lax.axis_size("expert")
    token_count, choice_count = routes.shape
    capacity = min(token_count, 2 * token_count * choice_count // groups)
    columns = tokens
    latent = jnp.dot(
        columns,
        lax.all_gather(enc_weight, "expert", axis=0, tiled=True),
        preferred_element_type=jnp.float32,
    ).astype(jnp.bfloat16)
    payload = lax.all_gather(latent, "hidden", axis=1, tiled=True)
    chosen = routes.reshape(-1)
    onehot = (chosen[:, None] == jnp.arange(groups, dtype=jnp.int32)[None, :]).astype(jnp.int32)
    position = jnp.sum((jnp.cumsum(onehot, axis=0) - onehot) * onehot, axis=1)
    target = chosen * capacity + position
    source_row = jnp.arange(token_count * choice_count, dtype=jnp.int32) // choice_count
    payload_width = payload.shape[1]
    outgoing = (
        jnp.zeros((groups * capacity, payload_width), jnp.bfloat16)
        .at[target]
        .set(payload[source_row])
    )
    outgoing = outgoing.reshape(groups, capacity, payload_width)
    gate_matrix = gate_weight[0]
    up_matrix = up_weight[0]
    down_matrix = down_weight[0]
    arrived = lax.all_to_all(outgoing, "expert", split_axis=0, concat_axis=0, tiled=True)
    slot_count = arrived.shape[1]
    inputs = arrived.reshape(groups * slot_count, arrived.shape[2])
    gate_part = jnp.dot(inputs, gate_matrix, preferred_element_type=jnp.float32)
    up_part = jnp.dot(inputs, up_matrix, preferred_element_type=jnp.float32)
    activation = (jax.nn.silu(gate_part) * up_part).astype(jnp.bfloat16)
    answer = jnp.dot(
        lax.all_gather(activation, "hidden", axis=1, tiled=True),
        down_matrix,
        preferred_element_type=jnp.float32,
    ).astype(jnp.bfloat16)
    answer = answer.reshape(groups, slot_count, down_matrix.shape[1])
    returned_rows = lax.all_to_all(answer, "expert", split_axis=0, concat_axis=0, tiled=True)
    returned_rows = returned_rows.reshape(groups * capacity, returned_rows.shape[2])
    picked = returned_rows[target].astype(jnp.float32).reshape(token_count, choice_count, -1)
    combined = jnp.sum(picked * gates[:, :, None], axis=1).astype(jnp.bfloat16)
    combined_all = lax.all_gather(combined, "hidden", axis=1, tiled=True)
    columns = combined_all
    return jnp.dot(
        columns,
        lax.all_gather(dec_weight, "expert", axis=0, tiled=True),
        preferred_element_type=jnp.float32,
    ).astype(jnp.bfloat16)


CORES, LINES = 2, 2
MESH = pl.DeviceIdType.MESH


def layer_kernel(
    tokens_hbm, enc, routes, gates, gate_hbm, up_hbm, down_hbm, dec, out,
    tokens, gate, up, down, enc_all, dec_all, latents, own_pack, pack_all, shares, total, activation,
    answers, core_in, x_out, x_in, keep, y_out, y_in, z_out, z_in, combined,
    enc_recv, enc_send, lat_recv, lat_send, dec_recv, dec_send,
    pack_recv, pack_send,
    down_recv, down_send, core_recv, core_send, x_lat_recv, x_lat_send, core_lat_recv, core_lat_send, x_recv, x_send, y_recv, y_send,
    z_recv, z_send, last_recv, last_send, local_sem,
):
    groups = lax.axis_size("expert")
    depth = groups // (CORES * LINES)
    e = lax.axis_index("expert")
    h = lax.axis_index("hidden")
    c, y, z = e % CORES, (e // CORES) % LINES, e // (CORES * LINES)

    def at(zz, yy, cc):
        return (zz * LINES + yy) * CORES + cc

    orders = []
    for zz in range(depth):
        others = [o for o in range(depth) if o != zz]
        orders.append([zz] + sorted(others, key=lambda o: (abs(o - zz), o)))
    nearest = []
    for s in range(depth):
        pick = jnp.int32(orders[0][s])
        for zz in range(1, depth):
            pick = jnp.where(z == zz, orders[zz][s], pick)
        nearest.append(pick)

    def behind(s):
        return nearest[s]

    rows = tokens.shape[0]
    half = latents.shape[2]
    enc_rows = tokens.shape[1] // groups
    band = LINES * CORES * rows
    y_peer = (at(z, 1 - y, c), h)
    core_peer = (at(z, y, 1 - c), h)
    x_peer = (e, 1 - h)
    z_peers = [(at((z + s) % depth, y, c), h) for s in range(1, depth)]
    above = (at(jnp.minimum(z + 1, depth - 1), y, c), h)
    below = (at(jnp.maximum(z - 1, 0), y, c), h)
    has_above, has_below = z < depth - 1, z > 0

    waiting = []

    def send(src, dst, ssem, rsem, peer, when=None):
        copy = pltpu.make_async_remote_copy(
            src_ref=src, dst_ref=dst, send_sem=ssem, recv_sem=rsem,
            device_id=peer, device_id_type=MESH,
        )
        if when is None:
            copy.start()
        else:
            pl.when(when)(copy.start)
        waiting.append((copy, when))

    def arrive(dst, rsem):
        pltpu.make_async_copy(dst, dst, rsem).wait()

    barrier = pltpu.get_barrier_semaphore()
    peers = z_peers + [y_peer, core_peer, x_peer]
    for peer in peers:
        pl.semaphore_signal(barrier, inc=1, device_id=peer, device_id_type=MESH)
    pl.semaphore_wait(barrier, len(peers))

    class Gather:
        def __init__(self, own, block, rsem, ssem):
            self.own, self.block, self.rsem, self.ssem = own, block, rsem, ssem

        def forward(self, o, peer, slot, own=False, when=None):
            src = self.own if own else self.block(o)
            send(src, self.block(o), self.ssem.at[slot], self.rsem.at[o], peer, when)

        def wait(self, o):
            arrive(self.block(o), self.rsem.at[o])

        def start_z(self):
            self.forward(e, above, 0, True, has_above)
            self.forward(e, below, 1, True, has_below)

        def start_y(self):
            self.forward(e, y_peer, depth + 1, True)
            self.forward(e, core_peer, 2 * depth + 1, True)

        def from_z(self, s):
            zz = nearest[s]
            o = at(zz, y, c)
            self.wait(o)
            self.forward(o, above, s + 1, False, jnp.logical_and(zz < z, has_above))
            self.forward(o, below, s + 1, False, jnp.logical_and(zz > z, has_below))
            self.forward(o, y_peer, depth + 1 + s)
            self.forward(o, core_peer, 2 * depth + 1 + s)
            return o

        def from_y(self, s):
            o = at(nearest[s], 1 - y, c)
            self.wait(o)
            self.forward(o, core_peer, 3 * depth + 1 + s)
            return o

        def from_core(self, s, yy):
            o = at(nearest[s], yy, 1 - c)
            self.wait(o)
            return o

    def lat_block(o):
        return latents.at[h, pl.ds(pl.multiple_of(o * rows, rows), rows)]

    class LatentGather(Gather):
        def start_y(self):
            Gather.start_y(self)
            send(lat(h, e), lat(h, e), x_lat_send.at[0], x_lat_recv.at[e], x_peer)

        def from_z(self, s):
            o = Gather.from_z(self, s)
            send(lat(h, o), lat(h, o), x_lat_send.at[s], x_lat_recv.at[o], x_peer)

        def from_y(self, s):
            o = Gather.from_y(self, s)
            send(lat(h, o), lat(h, o), x_lat_send.at[depth + s], x_lat_recv.at[o], x_peer)

    enc_gather = Gather(enc, lambda o: enc_all.at[o], enc_recv, enc_send)
    dec_gather = Gather(dec, lambda o: dec_all.at[o], dec_recv, dec_send)
    pack_gather = Gather(own_pack, lambda o: pack_all.at[o], pack_recv, pack_send)
    enc_gather.start_z()
    enc_gather.start_y()

    local = [
        pltpu.make_async_copy(tokens_hbm, tokens, local_sem.at[0]),
        pltpu.make_async_copy(gate_hbm.at[0], gate, local_sem.at[1]),
        pltpu.make_async_copy(up_hbm.at[0], up, local_sem.at[2]),
    ]
    for copy in local:
        copy.start()
    part = down.shape[1]
    own_down = pltpu.make_async_copy(
        down_hbm.at[0, pl.ds(pl.multiple_of(h * part, part), part)], down.at[h], local_sem.at[3]
    )
    own_down.start()
    send(
        down_hbm.at[0, pl.ds(pl.multiple_of((1 - h) * part, part), part)],
        down.at[h], down_send.at[0], down_recv.at[0], x_peer,
    )

    local[0].wait()

    def enc_dot(o, block):
        columns = pl.ds(pl.multiple_of(o * enc_rows, enc_rows), enc_rows)
        return jnp.dot(tokens[:, columns], block, preferred_element_type=jnp.float32)

    lane = lax.broadcasted_iota(jnp.int32, (rows, 128), 1)
    weight = jnp.zeros((rows, 128), jnp.float32)
    for k in range(routes.shape[1]):
        weight += jnp.where(routes[:, k : k + 1] == lane % groups, gates[:, k : k + 1], 0.0)
    first = weight.astype(jnp.bfloat16).astype(jnp.float32)
    second = (weight - first).astype(jnp.bfloat16).astype(jnp.float32)
    piece = jnp.where(lane < groups, first, jnp.where(lane < 2 * groups, second, weight - first - second))
    own_pack[...] = piece.astype(jnp.bfloat16)

    def take_shares(o, block):
        mine = jnp.logical_and(lane % groups == e, lane < 3 * groups)
        summed = jnp.sum(jnp.where(mine, block.astype(jnp.float32), 0.0), axis=1, keepdims=True)
        start = pl.multiple_of(o * rows, rows)
        shares[pl.ds(start, rows), :] = jnp.broadcast_to(summed, (rows, 128))

    total[...] = enc_dot(e, enc[...])
    take_shares(e, own_pack[...])

    def landed(o):
        total[...] += enc_dot(o, enc_all[o])

    for s in range(1, depth + 1):
        if s < depth:
            o = enc_gather.from_z(s)
            if s == depth - 1:
                dec_gather.start_z()
            landed(o)
        landed(enc_gather.from_y(s - 1))
    for yy in (y, 1 - y):
        for s in range(depth):
            landed(enc_gather.from_core(s, yy))

    def lat(hh, o):
        return latents.at[hh, pl.ds(pl.multiple_of(o * rows, rows), rows)]

    lat_gather = LatentGather(lat_block(e), lat_block, lat_recv, lat_send)
    latents[h, pl.ds(pl.multiple_of(e * rows, rows), rows), :] = total[...].astype(jnp.bfloat16)
    lat_gather.start_z()
    lat_gather.start_y()
    pack_gather.start_z()
    pack_gather.start_y()

    def lat_x(s):
        for k, yy in enumerate((y, 1 - y)):
            o = at(nearest[s], yy, c)
            arrive(lat(1 - h, o), x_lat_recv.at[o])
            send(lat(1 - h, o), lat(1 - h, o), core_lat_send.at[k * depth + s], core_lat_recv.at[o], core_peer)

    def lat_core(s):
        for yy in (y, 1 - y):
            o = lat_gather.from_core(s, yy)
            arrive(lat(1 - h, o), core_lat_recv.at[o])
            pack_gather.from_core(s, yy)
            take_shares(o, pack_all[o])

    tile = 256

    def experts(s):
        start = pl.multiple_of(behind(s) * band, band)

        @pl.loop(0, gate.shape[1] // tile)
        def _(n):
            columns = pl.ds(pl.multiple_of(n * tile, tile), tile)
            low, high = latents[0, pl.ds(start, band), :], latents[1, pl.ds(start, band), :]
            g = jnp.dot(low, gate[:half, columns], preferred_element_type=jnp.float32)
            g += jnp.dot(high, gate[half:, columns], preferred_element_type=jnp.float32)
            u = jnp.dot(low, up[:half, columns], preferred_element_type=jnp.float32)
            u += jnp.dot(high, up[half:, columns], preferred_element_type=jnp.float32)
            activation[:, columns] = (g / (1.0 + jnp.exp(-g)) * u).astype(jnp.bfloat16)

        for hh in range(2):
            @pl.loop(0, half // tile)
            def _(n):
                columns = pl.ds(pl.multiple_of(n * tile, tile), tile)
                a = jnp.dot(activation[...], down[hh, :, columns], preferred_element_type=jnp.float32)
                a = (a * shares[pl.ds(start, band), 0:1]).astype(jnp.bfloat16)
                for b in range(LINES * CORES):
                    answers[s, b, hh, :, columns] = a[b * rows : (b + 1) * rows]

        for yy in range(LINES):
            send(
                answers.at[s, yy * CORES + 1 - c], core_in.at[s, yy],
                core_send.at[s, yy], core_recv.at[s, yy], core_peer,
            )

    def sum_cores(s):
        for yy in range(LINES):
            arrive(core_in.at[s, yy], core_recv.at[s, yy])
            mine = yy * CORES + c
            other = answers[s, mine, 1 - h].astype(jnp.float32)
            x_out[s, yy] = (other + core_in[s, yy, 1 - h].astype(jnp.float32)).astype(jnp.bfloat16)
        send(x_out.at[s], x_in.at[s], x_send.at[s], x_recv.at[s], x_peer)
        for yy in range(LINES):
            mine = yy * CORES + c
            keep[s, yy] = answers[s, mine, h].astype(jnp.float32) + core_in[s, yy, h].astype(jnp.float32)

    def sum_x(s):
        arrive(x_in.at[s], x_recv.at[s])
        y_out[s] = (keep[s, 1 - y] + x_in[s, 1 - y].astype(jnp.float32)).astype(jnp.bfloat16)
        send(y_out.at[s], y_in.at[s], y_send.at[s], y_recv.at[s], y_peer)
        keep[s, y] = keep[s, y] + x_in[s, y].astype(jnp.float32)

    def sum_y(s):
        arrive(y_in.at[s], y_recv.at[s])
        total = keep[s, y] + y_in[s].astype(jnp.float32)
        if s == 0:
            keep[s, y] = total
        else:
            z_out[s] = total.astype(jnp.bfloat16)
            peer = (at(behind(s), y, c), h)
            send(z_out.at[s], z_in.at[z], z_send.at[s], z_recv.at[z], peer)

    def pack_z(s):
        take_shares(pack_gather.from_z(s), pack_all[at(nearest[s], y, c)])

    def pack_y(s):
        take_shares(pack_gather.from_y(s), pack_all[at(nearest[s], 1 - y, c)])

    for s in range(1, depth + 1):
        if s < depth:
            lat_gather.from_z(s)
        lat_gather.from_y(s - 1)
        if s < depth:
            pack_z(s)
        pack_y(s - 1)
    dec_gather.start_y()
    local[1].wait()
    local[2].wait()
    own_down.wait()
    arrive(down.at[1 - h], down_recv.at[0])
    for s in range(depth):
        lat_x(s)
        lat_core(s)
        experts(s)
        if s >= 1:
            sum_cores(s - 1)
            dec_gather.from_z(s)
        if s >= 2:
            sum_x(s - 2)
        if s >= 3:
            sum_y(s - 3)
    for s in range(depth, depth + 3):
        if s - 1 < depth:
            sum_cores(s - 1)
        if s - 2 < depth:
            sum_x(s - 2)
        if s - 3 < depth:
            sum_y(s - 3)
        if s < depth + 2:
            dec_gather.from_y(2 * (s - depth))
            dec_gather.from_y(2 * (s - depth) + 1)
    final = keep[0, y]
    for s in range(1, depth):
        arrive(z_in.at[nearest[s]], z_recv.at[nearest[s]])
        final += z_in[nearest[s]].astype(jnp.float32)
    combined[h] = final.astype(jnp.bfloat16)
    send(combined.at[h], combined.at[h], last_send.at[0], last_recv.at[0], x_peer)
    for s in range(depth):
        for yy in (y, 1 - y):
            dec_gather.from_core(s, yy)
    dec_all[e] = dec[...]
    arrive(combined.at[1 - h], last_recv.at[0])

    per = groups // 2

    @pl.loop(0, out.shape[1] // tile)
    def _(n):
        columns = pl.ds(pl.multiple_of(n * tile, tile), tile)
        low = dec_all[:per, :, columns].reshape(half, tile)
        high = dec_all[per:, :, columns].reshape(half, tile)
        m = jnp.dot(combined[0], low, preferred_element_type=jnp.float32)
        m += jnp.dot(combined[1], high, preferred_element_type=jnp.float32)
        out[:, columns] = m.astype(jnp.bfloat16)

    for copy, when in waiting:
        if when is None:
            copy.wait_send()
        else:
            pl.when(when)(copy.wait_send)


def whole_layer(tokens, enc_weight, routes, gates, gate_weight, up_weight, down_weight, dec_weight):
    groups = lax.axis_size("expert")
    depth = groups // (CORES * LINES)
    rows, width = tokens.shape
    half = enc_weight.shape[1]
    hidden = gate_weight.shape[2]
    bf, f32 = jnp.bfloat16, jnp.float32
    band = LINES * CORES
    anywhere = pl.BlockSpec(memory_space=pl.ANY)
    vmem = pl.BlockSpec(memory_space=pltpu.VMEM)
    dma = pltpu.SemaphoreType.DMA
    scratch = [
        pltpu.VMEM((rows, width), bf),
        pltpu.VMEM(gate_weight.shape[1:], bf),
        pltpu.VMEM(up_weight.shape[1:], bf),
        pltpu.VMEM((2, hidden, half), bf),
        pltpu.VMEM((groups, *enc_weight.shape), bf),
        pltpu.VMEM((groups, *dec_weight.shape), bf),
        pltpu.VMEM((2, groups * rows, half), bf),
        pltpu.VMEM((rows, 128), bf),
        pltpu.VMEM((groups, rows, 128), bf),
        pltpu.VMEM((groups * rows, 128), f32),
        pltpu.VMEM((rows, half), f32),
        pltpu.VMEM((band * rows, hidden), bf),
        pltpu.VMEM((depth, band, 2, rows, half), bf),
        pltpu.VMEM((depth, LINES, 2, rows, half), bf),
        pltpu.VMEM((depth, LINES, rows, half), bf),
        pltpu.VMEM((depth, LINES, rows, half), bf),
        pltpu.VMEM((depth, LINES, rows, half), f32),
        pltpu.VMEM((depth, rows, half), bf),
        pltpu.VMEM((depth, rows, half), bf),
        pltpu.VMEM((depth, rows, half), bf),
        pltpu.VMEM((depth, rows, half), bf),
        pltpu.VMEM((2, rows, half), bf),
        *[dma((groups,)), dma((4 * depth + 1,))] * 4,
        dma((1,)), dma((1,)),
        dma((depth, LINES)), dma((depth, LINES)),
        dma((groups,)), dma((2 * depth,)), dma((groups,)), dma((2 * depth,)),
        dma((depth,)), dma((depth,)), dma((depth,)), dma((depth,)), dma((depth,)), dma((depth,)),
        dma((1,)), dma((1,)), dma((4,)),
    ]
    return pl.pallas_call(
        layer_kernel,
        out_shape=jax.ShapeDtypeStruct((rows, dec_weight.shape[1]), bf),
        in_specs=[anywhere, vmem, vmem, vmem, anywhere, anywhere, anywhere, vmem],
        out_specs=vmem,
        scratch_shapes=scratch,
        compiler_params=pltpu.CompilerParams(
            collective_id=0, has_side_effects=True, vmem_limit_bytes=60 * 1024 * 1024
        ),
    )(tokens, enc_weight, routes, gates, gate_weight, up_weight, down_weight, dec_weight)


def on_device(tokens, enc_weight, routes, *rest):
    token_count, choice_count = routes.shape
    plan = whole_layer if 2 * choice_count >= lax.axis_size("expert") else exchange_slots
    return plan(tokens, enc_weight, routes, *rest)


def solution(mesh):
    in_specs = (
        P("expert", None),
        P("expert", "hidden"),
        P("expert", None),
        P("expert", None),
        P("expert", None, "hidden"),
        P("expert", None, "hidden"),
        P("expert", None, "hidden"),
        P("expert", "hidden"),
    )
    out_specs = P("expert", "hidden")
    return jax.shard_map(
        on_device, mesh=mesh, in_specs=in_specs, out_specs=out_specs, check_vma=False
    )
```

```python
import jax
import jax.numpy as jnp
from jax import lax
from jax.experimental import pallas as pl
from jax.experimental.pallas import tpu as pltpu
from jax.sharding import PartitionSpec as P


def exchange_slots(tokens, enc_weight, routes, gates, gate_weight, up_weight, down_weight, dec_weight):
    groups = lax.axis_size("expert")
    token_count, choice_count = routes.shape
    capacity = min(token_count, 2 * token_count * choice_count // groups)
    columns = tokens
    latent = jnp.dot(
        columns,
        lax.all_gather(enc_weight, "expert", axis=0, tiled=True),
        preferred_element_type=jnp.float32,
    ).astype(jnp.bfloat16)
    payload = lax.all_gather(latent, "hidden", axis=1, tiled=True)
    chosen = routes.reshape(-1)
    onehot = (chosen[:, None] == jnp.arange(groups, dtype=jnp.int32)[None, :]).astype(jnp.int32)
    position = jnp.sum((jnp.cumsum(onehot, axis=0) - onehot) * onehot, axis=1)
    target = chosen * capacity + position
    source_row = jnp.arange(token_count * choice_count, dtype=jnp.int32) // choice_count
    payload_width = payload.shape[1]
    outgoing = (
        jnp.zeros((groups * capacity, payload_width), jnp.bfloat16)
        .at[target]
        .set(payload[source_row])
    )
    outgoing = outgoing.reshape(groups, capacity, payload_width)
    gate_matrix = gate_weight[0]
    up_matrix = up_weight[0]
    down_matrix = down_weight[0]
    arrived = lax.all_to_all(outgoing, "expert", split_axis=0, concat_axis=0, tiled=True)
    slot_count = arrived.shape[1]
    inputs = arrived.reshape(groups * slot_count, arrived.shape[2])
    gate_part = jnp.dot(inputs, gate_matrix, preferred_element_type=jnp.float32)
    up_part = jnp.dot(inputs, up_matrix, preferred_element_type=jnp.float32)
    activation = (jax.nn.silu(gate_part) * up_part).astype(jnp.bfloat16)
    answer = jnp.dot(
        lax.all_gather(activation, "hidden", axis=1, tiled=True),
        down_matrix,
        preferred_element_type=jnp.float32,
    ).astype(jnp.bfloat16)
    answer = answer.reshape(groups, slot_count, down_matrix.shape[1])
    returned_rows = lax.all_to_all(answer, "expert", split_axis=0, concat_axis=0, tiled=True)
    returned_rows = returned_rows.reshape(groups * capacity, returned_rows.shape[2])
    picked = returned_rows[target].astype(jnp.float32).reshape(token_count, choice_count, -1)
    combined = jnp.sum(picked * gates[:, :, None], axis=1).astype(jnp.bfloat16)
    combined_all = lax.all_gather(combined, "hidden", axis=1, tiled=True)
    columns = combined_all
    return jnp.dot(
        columns,
        lax.all_gather(dec_weight, "expert", axis=0, tiled=True),
        preferred_element_type=jnp.float32,
    ).astype(jnp.bfloat16)


CORES, LINES = 2, 2
MESH = pl.DeviceIdType.MESH


def layer_kernel(
    tokens_hbm, enc, routes, gates, gate_hbm, up_hbm, down_hbm, dec, out,
    tokens, gate, up, down, enc_all, dec_all, latents, own_pack, pack_all, shares, total, mixed, activation,
    answers, core_in, x_out, x_in, keep, y_out, y_in, z_out, z_in, combined,
    enc_recv, enc_send, lat_recv, lat_send, dec_recv, dec_send,
    pack_recv, pack_send,
    down_recv, down_send, core_recv, core_send, x_lat_recv, x_lat_send, core_lat_recv, core_lat_send, x_recv, x_send, y_recv, y_send,
    z_recv, z_send, last_recv, last_send, local_sem,
):
    groups = lax.axis_size("expert")
    depth = groups // (CORES * LINES)
    e = lax.axis_index("expert")
    h = lax.axis_index("hidden")
    c, y, z = e % CORES, (e // CORES) % LINES, e // (CORES * LINES)

    def at(zz, yy, cc):
        return (zz * LINES + yy) * CORES + cc

    orders = []
    for zz in range(depth):
        others = [o for o in range(depth) if o != zz]
        orders.append([zz] + sorted(others, key=lambda o: (abs(o - zz), o)))
    nearest = []
    for s in range(depth):
        pick = jnp.int32(orders[0][s])
        for zz in range(1, depth):
            pick = jnp.where(z == zz, orders[zz][s], pick)
        nearest.append(pick)

    def behind(s):
        return nearest[s]

    rows = tokens.shape[0]
    half = latents.shape[2]
    enc_rows = tokens.shape[1] // groups
    band = LINES * CORES * rows
    y_peer = (at(z, 1 - y, c), h)
    core_peer = (at(z, y, 1 - c), h)
    x_peer = (e, 1 - h)
    z_peers = [(at((z + s) % depth, y, c), h) for s in range(1, depth)]
    above = (at(jnp.minimum(z + 1, depth - 1), y, c), h)
    below = (at(jnp.maximum(z - 1, 0), y, c), h)
    has_above, has_below = z < depth - 1, z > 0

    waiting = []

    def send(src, dst, ssem, rsem, peer, when=None):
        copy = pltpu.make_async_remote_copy(
            src_ref=src, dst_ref=dst, send_sem=ssem, recv_sem=rsem,
            device_id=peer, device_id_type=MESH,
        )
        if when is None:
            copy.start()
        else:
            pl.when(when)(copy.start)
        waiting.append((copy, when))

    def arrive(dst, rsem):
        pltpu.make_async_copy(dst, dst, rsem).wait()

    barrier = pltpu.get_barrier_semaphore()
    peers = z_peers + [y_peer, core_peer, x_peer]
    for peer in peers:
        pl.semaphore_signal(barrier, inc=1, device_id=peer, device_id_type=MESH)
    pl.semaphore_wait(barrier, len(peers))

    class Gather:
        def __init__(self, own, block, rsem, ssem):
            self.own, self.block, self.rsem, self.ssem = own, block, rsem, ssem

        def forward(self, o, peer, slot, own=False, when=None):
            src = self.own if own else self.block(o)
            send(src, self.block(o), self.ssem.at[slot], self.rsem.at[o], peer, when)

        def wait(self, o):
            arrive(self.block(o), self.rsem.at[o])

        def start_z(self):
            self.forward(e, above, 0, True, has_above)
            self.forward(e, below, 1, True, has_below)

        def start_y(self):
            self.forward(e, y_peer, depth + 1, True)
            self.forward(e, core_peer, 2 * depth + 1, True)

        def from_z(self, s):
            zz = nearest[s]
            o = at(zz, y, c)
            self.wait(o)
            self.forward(o, above, s + 1, False, jnp.logical_and(zz < z, has_above))
            self.forward(o, below, s + 1, False, jnp.logical_and(zz > z, has_below))
            self.forward(o, y_peer, depth + 1 + s)
            self.forward(o, core_peer, 2 * depth + 1 + s)
            return o

        def from_y(self, s):
            o = at(nearest[s], 1 - y, c)
            self.wait(o)
            self.forward(o, core_peer, 3 * depth + 1 + s)
            return o

        def from_core(self, s, yy):
            o = at(nearest[s], yy, 1 - c)
            self.wait(o)
            return o

    def lat_block(o):
        return latents.at[h, pl.ds(pl.multiple_of(o * rows, rows), rows)]

    class LatentGather(Gather):
        def start_y(self):
            Gather.start_y(self)
            send(lat(h, e), lat(h, e), x_lat_send.at[0], x_lat_recv.at[e], x_peer)

        def from_z(self, s):
            o = Gather.from_z(self, s)
            send(lat(h, o), lat(h, o), x_lat_send.at[s], x_lat_recv.at[o], x_peer)

        def from_y(self, s):
            o = Gather.from_y(self, s)
            send(lat(h, o), lat(h, o), x_lat_send.at[depth + s], x_lat_recv.at[o], x_peer)

    enc_gather = Gather(enc, lambda o: enc_all.at[o], enc_recv, enc_send)
    dec_gather = Gather(dec, lambda o: dec_all.at[o], dec_recv, dec_send)
    pack_gather = Gather(own_pack, lambda o: pack_all.at[o], pack_recv, pack_send)
    enc_gather.start_z()
    enc_gather.start_y()

    local = [
        pltpu.make_async_copy(tokens_hbm, tokens, local_sem.at[0]),
        pltpu.make_async_copy(gate_hbm.at[0], gate, local_sem.at[1]),
        pltpu.make_async_copy(up_hbm.at[0], up, local_sem.at[2]),
    ]
    for copy in local:
        copy.start()
    part = down.shape[1]
    own_down = pltpu.make_async_copy(
        down_hbm.at[0, pl.ds(pl.multiple_of(h * part, part), part)], down.at[h], local_sem.at[3]
    )
    own_down.start()
    send(
        down_hbm.at[0, pl.ds(pl.multiple_of((1 - h) * part, part), part)],
        down.at[h], down_send.at[0], down_recv.at[0], x_peer,
    )

    local[0].wait()

    def enc_dot(o, block):
        columns = pl.ds(pl.multiple_of(o * enc_rows, enc_rows), enc_rows)
        return jnp.dot(tokens[:, columns], block, preferred_element_type=jnp.float32)

    lane = lax.broadcasted_iota(jnp.int32, (rows, 128), 1)
    weight = jnp.zeros((rows, 128), jnp.float32)
    for k in range(routes.shape[1]):
        weight += jnp.where(routes[:, k : k + 1] == lane % groups, gates[:, k : k + 1], 0.0)
    first = weight.astype(jnp.bfloat16).astype(jnp.float32)
    second = (weight - first).astype(jnp.bfloat16).astype(jnp.float32)
    piece = jnp.where(lane < groups, first, jnp.where(lane < 2 * groups, second, weight - first - second))
    own_pack[...] = piece.astype(jnp.bfloat16)

    def take_shares(o, block):
        mine = jnp.logical_and(lane % groups == e, lane < 3 * groups)
        summed = jnp.sum(jnp.where(mine, block.astype(jnp.float32), 0.0), axis=1, keepdims=True)
        start = pl.multiple_of(o * rows, rows)
        shares[pl.ds(start, rows), :] = jnp.broadcast_to(summed, (rows, 128))

    total[...] = enc_dot(e, enc[...])
    take_shares(e, own_pack[...])

    def landed(o):
        total[...] += enc_dot(o, enc_all[o])

    for s in range(1, depth + 1):
        if s < depth:
            o = enc_gather.from_z(s)
            if s == depth - 1:
                dec_gather.start_z()
            landed(o)
        landed(enc_gather.from_y(s - 1))
    for yy in (y, 1 - y):
        for s in range(depth):
            landed(enc_gather.from_core(s, yy))

    def lat(hh, o):
        return latents.at[hh, pl.ds(pl.multiple_of(o * rows, rows), rows)]

    lat_gather = LatentGather(lat_block(e), lat_block, lat_recv, lat_send)
    latents[h, pl.ds(pl.multiple_of(e * rows, rows), rows), :] = total[...].astype(jnp.bfloat16)
    lat_gather.start_z()
    lat_gather.start_y()
    pack_gather.start_z()
    pack_gather.start_y()

    def lat_x(s):
        for k, yy in enumerate((y, 1 - y)):
            o = at(nearest[s], yy, c)
            arrive(lat(1 - h, o), x_lat_recv.at[o])
            send(lat(1 - h, o), lat(1 - h, o), core_lat_send.at[k * depth + s], core_lat_recv.at[o], core_peer)

    def lat_core(s):
        for yy in (y, 1 - y):
            o = lat_gather.from_core(s, yy)
            arrive(lat(1 - h, o), core_lat_recv.at[o])
            pack_gather.from_core(s, yy)
            take_shares(o, pack_all[o])

    tile = 256

    def gate_up(s, slot):
        start = pl.multiple_of(behind(s) * band, band)

        @pl.loop(0, gate.shape[1] // tile)
        def _(n):
            columns = pl.ds(pl.multiple_of(n * tile, tile), tile)
            low, high = latents[0, pl.ds(start, band), :], latents[1, pl.ds(start, band), :]
            g = jnp.dot(low, gate[:half, columns], preferred_element_type=jnp.float32)
            g += jnp.dot(high, gate[half:, columns], preferred_element_type=jnp.float32)
            u = jnp.dot(low, up[:half, columns], preferred_element_type=jnp.float32)
            u += jnp.dot(high, up[half:, columns], preferred_element_type=jnp.float32)
            activation[slot, :, columns] = (g / (1.0 + jnp.exp(-g)) * u).astype(jnp.bfloat16)

    def down_rows(s, slot, cc):
        blocks = [yy * CORES + cc for yy in range(LINES)]
        for hh in range(2):
            @pl.loop(0, half // tile)
            def _(n):
                columns = pl.ds(pl.multiple_of(n * tile, tile), tile)
                picked = [activation[slot, pl.ds(pl.multiple_of(b * rows, rows), rows), :] for b in blocks]
                a = jnp.dot(
                    jnp.concatenate(picked, axis=0), down[hh, :, columns],
                    preferred_element_type=jnp.float32,
                )
                for k, b in enumerate(blocks):
                    start = pl.multiple_of(behind(s) * band + b * rows, rows)
                    share = shares[pl.ds(start, rows), 0:1]
                    answers[s, b, hh, :, columns] = (a[k * rows : (k + 1) * rows] * share).astype(jnp.bfloat16)

    def answer_rows(s, slot):
        down_rows(s, slot, 1 - c)
        for yy in range(LINES):
            send(
                answers.at[s, yy * CORES + 1 - c], core_in.at[s, yy],
                core_send.at[s, yy], core_recv.at[s, yy], core_peer,
            )
        down_rows(s, slot, c)

    def sum_cores(s):
        for yy in range(LINES):
            arrive(core_in.at[s, yy], core_recv.at[s, yy])
        for yy in (1 - y, y):
            mine = yy * CORES + c
            other = answers[s, mine, 1 - h].astype(jnp.float32)
            x_out[s, yy] = (other + core_in[s, yy, 1 - h].astype(jnp.float32)).astype(jnp.bfloat16)
            send(x_out.at[s, yy], x_in.at[s, yy], x_send.at[s, yy], x_recv.at[s, yy], x_peer)
        for yy in range(LINES):
            mine = yy * CORES + c
            keep[s, yy] = answers[s, mine, h].astype(jnp.float32) + core_in[s, yy, h].astype(jnp.float32)

    def sum_x(s):
        arrive(x_in.at[s, 1 - y], x_recv.at[s, 1 - y])
        y_out[s] = (keep[s, 1 - y] + x_in[s, 1 - y].astype(jnp.float32)).astype(jnp.bfloat16)
        send(y_out.at[s], y_in.at[s], y_send.at[s], y_recv.at[s], y_peer)
        arrive(x_in.at[s, y], x_recv.at[s, y])
        keep[s, y] = keep[s, y] + x_in[s, y].astype(jnp.float32)

    def sum_y(s):
        arrive(y_in.at[s], y_recv.at[s])
        total = keep[s, y] + y_in[s].astype(jnp.float32)
        if s == 0:
            keep[s, y] = total
        else:
            z_out[s] = total.astype(jnp.bfloat16)
            peer = (at(behind(s), y, c), h)
            send(z_out.at[s], z_in.at[z], z_send.at[s], z_recv.at[z], peer)

    def pack_z(s):
        take_shares(pack_gather.from_z(s), pack_all[at(nearest[s], y, c)])

    def pack_y(s):
        take_shares(pack_gather.from_y(s), pack_all[at(nearest[s], 1 - y, c)])

    for s in range(1, depth + 1):
        if s < depth:
            lat_gather.from_z(s)
        lat_gather.from_y(s - 1)
        if s < depth:
            pack_z(s)
        pack_y(s - 1)
    dec_gather.start_y()
    local[1].wait()
    local[2].wait()
    own_down.wait()
    arrive(down.at[1 - h], down_recv.at[0])
    last = depth - 1
    dec_gather.from_z(1)
    lat_x(0)
    lat_core(0)
    gate_up(0, 0)
    lat_x(1)
    lat_core(1)
    for s in range(1, depth):
        gate_up(s, 1)
        if s < last:
            lat_x(s + 1)
        answer_rows(s, 1)
        sum_cores(s)
        if s < last:
            lat_core(s + 1)
            dec_gather.from_z(s + 1)
        if s >= 2:
            sum_x(s - 1)
        if s >= 3:
            sum_y(s - 2)
    answer_rows(0, 0)
    sum_cores(0)
    if last >= 2:
        sum_y(last - 1)
    sum_x(last)
    for s in range(depth):
        dec_gather.from_y(s)
    sum_y(last)
    sum_x(0)
    final = jnp.zeros((rows, half), jnp.float32)
    for s in range(1, depth):
        arrive(z_in.at[nearest[s]], z_recv.at[nearest[s]])
        final += z_in[nearest[s]].astype(jnp.float32)
    total[...] = final
    for s in range(depth):
        for yy in (y, 1 - y):
            dec_gather.from_core(s, yy)
    dec_all[e] = dec[...]
    sum_y(0)
    combined[h] = (total[...] + keep[0, y]).astype(jnp.bfloat16)
    send(combined.at[h], combined.at[h], last_send.at[0], last_recv.at[0], x_peer)

    per = groups // 2

    def product(hh, columns):
        part = dec_all[pl.ds(pl.multiple_of(hh * per, per), per), :, columns].reshape(half, tile)
        return jnp.dot(combined[hh], part, preferred_element_type=jnp.float32)

    @pl.loop(0, out.shape[1] // tile)
    def _(n):
        columns = pl.ds(pl.multiple_of(n * tile, tile), tile)
        mixed[:, columns] = product(h, columns)

    arrive(combined.at[1 - h], last_recv.at[0])

    @pl.loop(0, out.shape[1] // tile)
    def _(n):
        columns = pl.ds(pl.multiple_of(n * tile, tile), tile)
        out[:, columns] = (mixed[:, columns] + product(1 - h, columns)).astype(jnp.bfloat16)

    for copy, when in waiting:
        if when is None:
            copy.wait_send()
        else:
            pl.when(when)(copy.wait_send)


def whole_layer(tokens, enc_weight, routes, gates, gate_weight, up_weight, down_weight, dec_weight):
    groups = lax.axis_size("expert")
    depth = groups // (CORES * LINES)
    rows, width = tokens.shape
    half = enc_weight.shape[1]
    hidden = gate_weight.shape[2]
    bf, f32 = jnp.bfloat16, jnp.float32
    band = LINES * CORES
    anywhere = pl.BlockSpec(memory_space=pl.ANY)
    vmem = pl.BlockSpec(memory_space=pltpu.VMEM)
    dma = pltpu.SemaphoreType.DMA
    scratch = [
        pltpu.VMEM((rows, width), bf),
        pltpu.VMEM(gate_weight.shape[1:], bf),
        pltpu.VMEM(up_weight.shape[1:], bf),
        pltpu.VMEM((2, hidden, half), bf),
        pltpu.VMEM((groups, *enc_weight.shape), bf),
        pltpu.VMEM((groups, *dec_weight.shape), bf),
        pltpu.VMEM((2, groups * rows, half), bf),
        pltpu.VMEM((rows, 128), bf),
        pltpu.VMEM((groups, rows, 128), bf),
        pltpu.VMEM((groups * rows, 128), f32),
        pltpu.VMEM((rows, half), f32),
        pltpu.VMEM((rows, dec_weight.shape[1]), f32),
        pltpu.VMEM((2, band * rows, hidden), bf),
        pltpu.VMEM((depth, band, 2, rows, half), bf),
        pltpu.VMEM((depth, LINES, 2, rows, half), bf),
        pltpu.VMEM((depth, LINES, rows, half), bf),
        pltpu.VMEM((depth, LINES, rows, half), bf),
        pltpu.VMEM((depth, LINES, rows, half), f32),
        pltpu.VMEM((depth, rows, half), bf),
        pltpu.VMEM((depth, rows, half), bf),
        pltpu.VMEM((depth, rows, half), bf),
        pltpu.VMEM((depth, rows, half), bf),
        pltpu.VMEM((2, rows, half), bf),
        *[dma((groups,)), dma((4 * depth + 1,))] * 4,
        dma((1,)), dma((1,)),
        dma((depth, LINES)), dma((depth, LINES)),
        dma((groups,)), dma((2 * depth,)), dma((groups,)), dma((2 * depth,)),
        dma((depth, LINES)), dma((depth, LINES)), dma((depth,)), dma((depth,)), dma((depth,)), dma((depth,)),
        dma((1,)), dma((1,)), dma((4,)),
    ]
    return pl.pallas_call(
        layer_kernel,
        out_shape=jax.ShapeDtypeStruct((rows, dec_weight.shape[1]), bf),
        in_specs=[anywhere, vmem, vmem, vmem, anywhere, anywhere, anywhere, vmem],
        out_specs=vmem,
        scratch_shapes=scratch,
        compiler_params=pltpu.CompilerParams(
            collective_id=0, has_side_effects=True, vmem_limit_bytes=60 * 1024 * 1024
        ),
    )(tokens, enc_weight, routes, gates, gate_weight, up_weight, down_weight, dec_weight)


def on_device(tokens, enc_weight, routes, *rest):
    token_count, choice_count = routes.shape
    plan = whole_layer if 2 * choice_count >= lax.axis_size("expert") else exchange_slots
    return plan(tokens, enc_weight, routes, *rest)


def solution(mesh):
    in_specs = (
        P("expert", None),
        P("expert", "hidden"),
        P("expert", None),
        P("expert", None),
        P("expert", None, "hidden"),
        P("expert", None, "hidden"),
        P("expert", None, "hidden"),
        P("expert", "hidden"),
    )
    out_specs = P("expert", "hidden")
    return jax.shard_map(
        on_device, mesh=mesh, in_specs=in_specs, out_specs=out_specs, check_vma=False
    )
```

```python
import jax
import jax.numpy as jnp
from jax import lax
from jax.experimental import pallas as pl
from jax.experimental.pallas import tpu as pltpu
from jax.sharding import PartitionSpec as P


def exchange_slots(tokens, enc_weight, routes, gates, gate_weight, up_weight, down_weight, dec_weight):
    groups = lax.axis_size("expert")
    token_count, choice_count = routes.shape
    capacity = min(token_count, 2 * token_count * choice_count // groups)
    columns = tokens
    latent = jnp.dot(
        columns,
        lax.all_gather(enc_weight, "expert", axis=0, tiled=True),
        preferred_element_type=jnp.float32,
    ).astype(jnp.bfloat16)
    payload = lax.all_gather(latent, "hidden", axis=1, tiled=True)
    chosen = routes.reshape(-1)
    onehot = (chosen[:, None] == jnp.arange(groups, dtype=jnp.int32)[None, :]).astype(jnp.int32)
    position = jnp.sum((jnp.cumsum(onehot, axis=0) - onehot) * onehot, axis=1)
    target = chosen * capacity + position
    source_row = jnp.arange(token_count * choice_count, dtype=jnp.int32) // choice_count
    payload_width = payload.shape[1]
    outgoing = (
        jnp.zeros((groups * capacity, payload_width), jnp.bfloat16)
        .at[target]
        .set(payload[source_row])
    )
    outgoing = outgoing.reshape(groups, capacity, payload_width)
    gate_matrix = gate_weight[0]
    up_matrix = up_weight[0]
    down_matrix = down_weight[0]
    arrived = lax.all_to_all(outgoing, "expert", split_axis=0, concat_axis=0, tiled=True)
    slot_count = arrived.shape[1]
    inputs = arrived.reshape(groups * slot_count, arrived.shape[2])
    gate_part = jnp.dot(inputs, gate_matrix, preferred_element_type=jnp.float32)
    up_part = jnp.dot(inputs, up_matrix, preferred_element_type=jnp.float32)
    activation = (jax.nn.silu(gate_part) * up_part).astype(jnp.bfloat16)
    answer = jnp.dot(
        lax.all_gather(activation, "hidden", axis=1, tiled=True),
        down_matrix,
        preferred_element_type=jnp.float32,
    ).astype(jnp.bfloat16)
    answer = answer.reshape(groups, slot_count, down_matrix.shape[1])
    returned_rows = lax.all_to_all(answer, "expert", split_axis=0, concat_axis=0, tiled=True)
    returned_rows = returned_rows.reshape(groups * capacity, returned_rows.shape[2])
    picked = returned_rows[target].astype(jnp.float32).reshape(token_count, choice_count, -1)
    combined = jnp.sum(picked * gates[:, :, None], axis=1).astype(jnp.bfloat16)
    combined_all = lax.all_gather(combined, "hidden", axis=1, tiled=True)
    columns = combined_all
    return jnp.dot(
        columns,
        lax.all_gather(dec_weight, "expert", axis=0, tiled=True),
        preferred_element_type=jnp.float32,
    ).astype(jnp.bfloat16)


CORES, LINES = 2, 2
MESH = pl.DeviceIdType.MESH


def layer_kernel(
    tokens_hbm, enc, routes, gates, gate_hbm, up_hbm, down_hbm, dec, out,
    tokens, gate, up, down, enc_all, dec_all, latents, own_pack, pack_all, shares, total, mixed, activation,
    answers, core_in, x_out, x_in, keep, y_out, y_in, z_out, z_in, combined,
    enc_recv, enc_send, lat_recv, lat_send, dec_recv, dec_send,
    pack_recv, pack_send,
    down_recv, down_send, core_recv, core_send, x_lat_recv, x_lat_send, core_lat_recv, core_lat_send, x_recv, x_send, y_recv, y_send,
    z_recv, z_send, last_recv, last_send, local_sem,
):
    groups = lax.axis_size("expert")
    depth = groups // (CORES * LINES)
    e = lax.axis_index("expert")
    h = lax.axis_index("hidden")
    c, y, z = e % CORES, (e // CORES) % LINES, e // (CORES * LINES)

    def at(zz, yy, cc):
        return (zz * LINES + yy) * CORES + cc

    orders = []
    for zz in range(depth):
        others = [o for o in range(depth) if o != zz]
        orders.append([zz] + sorted(others, key=lambda o: (abs(o - zz), o)))
    nearest = []
    for s in range(depth):
        pick = jnp.int32(orders[0][s])
        for zz in range(1, depth):
            pick = jnp.where(z == zz, orders[zz][s], pick)
        nearest.append(pick)

    def behind(s):
        return nearest[s]

    rows = tokens.shape[0]
    half = latents.shape[2]
    enc_rows = tokens.shape[1] // groups
    band = LINES * CORES * rows
    y_peer = (at(z, 1 - y, c), h)
    core_peer = (at(z, y, 1 - c), h)
    x_peer = (e, 1 - h)
    z_peers = [(at((z + s) % depth, y, c), h) for s in range(1, depth)]
    above = (at(jnp.minimum(z + 1, depth - 1), y, c), h)
    below = (at(jnp.maximum(z - 1, 0), y, c), h)
    has_above, has_below = z < depth - 1, z > 0

    waiting = []

    def send(src, dst, ssem, rsem, peer, when=None):
        copy = pltpu.make_async_remote_copy(
            src_ref=src, dst_ref=dst, send_sem=ssem, recv_sem=rsem,
            device_id=peer, device_id_type=MESH,
        )
        if when is None:
            copy.start()
        else:
            pl.when(when)(copy.start)
        waiting.append((copy, when))

    def arrive(dst, rsem):
        pltpu.make_async_copy(dst, dst, rsem).wait()

    barrier = pltpu.get_barrier_semaphore()
    peers = z_peers + [y_peer, core_peer, x_peer]
    for peer in peers:
        pl.semaphore_signal(barrier, inc=1, device_id=peer, device_id_type=MESH)
    pl.semaphore_wait(barrier, len(peers))

    class Gather:
        def __init__(self, own, block, rsem, ssem):
            self.own, self.block, self.rsem, self.ssem = own, block, rsem, ssem

        def forward(self, o, peer, slot, own=False, when=None):
            src = self.own if own else self.block(o)
            send(src, self.block(o), self.ssem.at[slot], self.rsem.at[o], peer, when)

        def wait(self, o):
            arrive(self.block(o), self.rsem.at[o])

        def start_z(self):
            self.forward(e, above, 0, True, has_above)
            self.forward(e, below, 1, True, has_below)

        def start_y(self):
            self.forward(e, y_peer, depth + 1, True)
            self.forward(e, core_peer, 2 * depth + 1, True)

        def from_z(self, s):
            zz = nearest[s]
            o = at(zz, y, c)
            self.wait(o)
            self.forward(o, above, s + 1, False, jnp.logical_and(zz < z, has_above))
            self.forward(o, below, s + 1, False, jnp.logical_and(zz > z, has_below))
            self.forward(o, y_peer, depth + 1 + s)
            self.forward(o, core_peer, 2 * depth + 1 + s)
            return o

        def from_y(self, s):
            o = at(nearest[s], 1 - y, c)
            self.wait(o)
            self.forward(o, core_peer, 3 * depth + 1 + s)
            return o

        def from_core(self, s, yy):
            o = at(nearest[s], yy, 1 - c)
            self.wait(o)
            return o

    def lat_block(o):
        return latents.at[h, pl.ds(pl.multiple_of(o * rows, rows), rows)]

    class LatentGather(Gather):
        def start_y(self):
            Gather.start_y(self)
            send(lat(h, e), lat(h, e), x_lat_send.at[0], x_lat_recv.at[e], x_peer)

        def from_z(self, s):
            o = Gather.from_z(self, s)
            send(lat(h, o), lat(h, o), x_lat_send.at[s], x_lat_recv.at[o], x_peer)

        def from_y(self, s):
            o = Gather.from_y(self, s)
            send(lat(h, o), lat(h, o), x_lat_send.at[depth + s], x_lat_recv.at[o], x_peer)

    enc_gather = Gather(enc, lambda o: enc_all.at[o], enc_recv, enc_send)
    dec_gather = Gather(dec, lambda o: dec_all.at[o], dec_recv, dec_send)
    pack_gather = Gather(own_pack, lambda o: pack_all.at[o], pack_recv, pack_send)
    enc_gather.start_z()
    enc_gather.start_y()

    local = [
        pltpu.make_async_copy(tokens_hbm, tokens, local_sem.at[0]),
        pltpu.make_async_copy(gate_hbm.at[0], gate, local_sem.at[1]),
        pltpu.make_async_copy(up_hbm.at[0], up, local_sem.at[2]),
    ]
    for copy in local:
        copy.start()
    part = down.shape[1]
    own_down = pltpu.make_async_copy(
        down_hbm.at[0, pl.ds(pl.multiple_of(h * part, part), part)], down.at[h], local_sem.at[3]
    )
    own_down.start()
    send(
        down_hbm.at[0, pl.ds(pl.multiple_of((1 - h) * part, part), part)],
        down.at[h], down_send.at[0], down_recv.at[0], x_peer,
    )

    local[0].wait()

    def enc_dot(o, block):
        columns = pl.ds(pl.multiple_of(o * enc_rows, enc_rows), enc_rows)
        return jnp.dot(tokens[:, columns], block, preferred_element_type=jnp.float32)

    lane = lax.broadcasted_iota(jnp.int32, (rows, 128), 1)
    weight = jnp.zeros((rows, 128), jnp.float32)
    for k in range(routes.shape[1]):
        weight += jnp.where(routes[:, k : k + 1] == lane % groups, gates[:, k : k + 1], 0.0)
    first = weight.astype(jnp.bfloat16).astype(jnp.float32)
    second = (weight - first).astype(jnp.bfloat16).astype(jnp.float32)
    piece = jnp.where(lane < groups, first, jnp.where(lane < 2 * groups, second, weight - first - second))
    own_pack[...] = piece.astype(jnp.bfloat16)

    def take_shares(o, block):
        mine = jnp.logical_and(lane % groups == e, lane < 3 * groups)
        summed = jnp.sum(jnp.where(mine, block.astype(jnp.float32), 0.0), axis=1, keepdims=True)
        start = pl.multiple_of(o * rows, rows)
        shares[pl.ds(start, rows), :] = jnp.broadcast_to(summed, (rows, 128))

    total[...] = enc_dot(e, enc[...])
    take_shares(e, own_pack[...])

    def landed(o):
        total[...] += enc_dot(o, enc_all[o])

    for s in range(1, depth + 1):
        if s < depth:
            o = enc_gather.from_z(s)
            if s == depth - 1:
                dec_gather.start_z()
            landed(o)
        landed(enc_gather.from_y(s - 1))
        landed(enc_gather.from_core(s - 1, y))
        if s >= 2:
            landed(enc_gather.from_core(s - 2, 1 - y))
    landed(enc_gather.from_core(depth - 1, 1 - y))

    def lat(hh, o):
        return latents.at[hh, pl.ds(pl.multiple_of(o * rows, rows), rows)]

    lat_gather = LatentGather(lat_block(e), lat_block, lat_recv, lat_send)
    latents[h, pl.ds(pl.multiple_of(e * rows, rows), rows), :] = total[...].astype(jnp.bfloat16)
    lat_gather.start_z()
    lat_gather.start_y()
    pack_gather.start_z()
    pack_gather.start_y()

    def lat_x(s):
        for k, yy in enumerate((y, 1 - y)):
            o = at(nearest[s], yy, c)
            arrive(lat(1 - h, o), x_lat_recv.at[o])
            send(lat(1 - h, o), lat(1 - h, o), core_lat_send.at[k * depth + s], core_lat_recv.at[o], core_peer)

    def lat_core(s):
        for yy in (y, 1 - y):
            o = lat_gather.from_core(s, yy)
            arrive(lat(1 - h, o), core_lat_recv.at[o])
            pack_gather.from_core(s, yy)
            take_shares(o, pack_all[o])

    tile = 256

    def gate_up(s, slot):
        start = pl.multiple_of(behind(s) * band, band)

        @pl.loop(0, gate.shape[1] // tile)
        def _(n):
            columns = pl.ds(pl.multiple_of(n * tile, tile), tile)
            low, high = latents[0, pl.ds(start, band), :], latents[1, pl.ds(start, band), :]
            g = jnp.dot(low, gate[:half, columns], preferred_element_type=jnp.float32)
            g += jnp.dot(high, gate[half:, columns], preferred_element_type=jnp.float32)
            u = jnp.dot(low, up[:half, columns], preferred_element_type=jnp.float32)
            u += jnp.dot(high, up[half:, columns], preferred_element_type=jnp.float32)
            activation[slot, :, columns] = (g / (1.0 + jnp.exp(-g)) * u).astype(jnp.bfloat16)

    def down_rows(s, slot, cc):
        blocks = [yy * CORES + cc for yy in range(LINES)]
        for hh in range(2):
            @pl.loop(0, half // tile)
            def _(n):
                columns = pl.ds(pl.multiple_of(n * tile, tile), tile)
                picked = [activation[slot, pl.ds(pl.multiple_of(b * rows, rows), rows), :] for b in blocks]
                a = jnp.dot(
                    jnp.concatenate(picked, axis=0), down[hh, :, columns],
                    preferred_element_type=jnp.float32,
                )
                for k, b in enumerate(blocks):
                    start = pl.multiple_of(behind(s) * band + b * rows, rows)
                    share = shares[pl.ds(start, rows), 0:1]
                    answers[s, b, hh, :, columns] = (a[k * rows : (k + 1) * rows] * share).astype(jnp.bfloat16)

    def answer_rows(s, slot):
        down_rows(s, slot, 1 - c)
        for yy in range(LINES):
            send(
                answers.at[s, yy * CORES + 1 - c], core_in.at[s, yy],
                core_send.at[s, yy], core_recv.at[s, yy], core_peer,
            )
        down_rows(s, slot, c)

    def sum_cores(s):
        for yy in range(LINES):
            arrive(core_in.at[s, yy], core_recv.at[s, yy])
        for yy in (1 - y, y):
            mine = yy * CORES + c
            other = answers[s, mine, 1 - h].astype(jnp.float32)
            x_out[s, yy] = (other + core_in[s, yy, 1 - h].astype(jnp.float32)).astype(jnp.bfloat16)
            send(x_out.at[s, yy], x_in.at[s, yy], x_send.at[s, yy], x_recv.at[s, yy], x_peer)
        for yy in range(LINES):
            mine = yy * CORES + c
            keep[s, yy] = answers[s, mine, h].astype(jnp.float32) + core_in[s, yy, h].astype(jnp.float32)

    def sum_x(s):
        arrive(x_in.at[s, 1 - y], x_recv.at[s, 1 - y])
        y_out[s] = (keep[s, 1 - y] + x_in[s, 1 - y].astype(jnp.float32)).astype(jnp.bfloat16)
        send(y_out.at[s], y_in.at[s], y_send.at[s], y_recv.at[s], y_peer)
        arrive(x_in.at[s, y], x_recv.at[s, y])
        keep[s, y] = keep[s, y] + x_in[s, y].astype(jnp.float32)

    def sum_y(s):
        arrive(y_in.at[s], y_recv.at[s])
        total = keep[s, y] + y_in[s].astype(jnp.float32)
        if s == 0:
            keep[s, y] = total
        else:
            z_out[s] = total.astype(jnp.bfloat16)
            peer = (at(behind(s), y, c), h)
            send(z_out.at[s], z_in.at[z], z_send.at[s], z_recv.at[z], peer)

    def pack_z(s):
        take_shares(pack_gather.from_z(s), pack_all[at(nearest[s], y, c)])

    def pack_y(s):
        take_shares(pack_gather.from_y(s), pack_all[at(nearest[s], 1 - y, c)])

    for s in range(1, depth + 1):
        if s < depth:
            lat_gather.from_z(s)
        lat_gather.from_y(s - 1)
        if s < depth:
            pack_z(s)
        pack_y(s - 1)
    dec_gather.start_y()
    local[1].wait()
    local[2].wait()
    own_down.wait()
    arrive(down.at[1 - h], down_recv.at[0])
    last = depth - 1
    dec_gather.from_z(1)
    lat_x(0)
    lat_core(0)
    gate_up(0, 0)
    lat_x(1)
    lat_core(1)
    for s in range(1, depth):
        gate_up(s, 1)
        if s < last:
            lat_x(s + 1)
        answer_rows(s, 1)
        sum_cores(s)
        if s < last:
            lat_core(s + 1)
        if s >= 2:
            sum_x(s - 1)
        if s >= 3:
            sum_y(s - 2)
        if s < last:
            dec_gather.from_z(s + 1)
    answer_rows(0, 0)
    sum_cores(0)
    if last >= 2:
        sum_y(last - 1)
    sum_x(last)
    for s in range(depth):
        dec_gather.from_y(s)
    sum_y(last)
    sum_x(0)
    final = jnp.zeros((rows, half), jnp.float32)
    for s in range(1, depth):
        arrive(z_in.at[nearest[s]], z_recv.at[nearest[s]])
        final += z_in[nearest[s]].astype(jnp.float32)
    total[...] = final
    for s in range(depth):
        for yy in (y, 1 - y):
            dec_gather.from_core(s, yy)
    dec_all[e] = dec[...]
    sum_y(0)
    combined[h] = (total[...] + keep[0, y]).astype(jnp.bfloat16)
    send(combined.at[h], combined.at[h], last_send.at[0], last_recv.at[0], x_peer)

    per = groups // 2

    def product(hh, columns):
        part = dec_all[pl.ds(pl.multiple_of(hh * per, per), per), :, columns].reshape(half, tile)
        return jnp.dot(combined[hh], part, preferred_element_type=jnp.float32)

    @pl.loop(0, out.shape[1] // tile)
    def _(n):
        columns = pl.ds(pl.multiple_of(n * tile, tile), tile)
        mixed[:, columns] = product(h, columns)

    arrive(combined.at[1 - h], last_recv.at[0])

    @pl.loop(0, out.shape[1] // tile)
    def _(n):
        columns = pl.ds(pl.multiple_of(n * tile, tile), tile)
        out[:, columns] = (mixed[:, columns] + product(1 - h, columns)).astype(jnp.bfloat16)

    for copy, when in waiting:
        if when is None:
            copy.wait_send()
        else:
            pl.when(when)(copy.wait_send)


def whole_layer(tokens, enc_weight, routes, gates, gate_weight, up_weight, down_weight, dec_weight):
    groups = lax.axis_size("expert")
    depth = groups // (CORES * LINES)
    rows, width = tokens.shape
    half = enc_weight.shape[1]
    hidden = gate_weight.shape[2]
    bf, f32 = jnp.bfloat16, jnp.float32
    band = LINES * CORES
    anywhere = pl.BlockSpec(memory_space=pl.ANY)
    vmem = pl.BlockSpec(memory_space=pltpu.VMEM)
    dma = pltpu.SemaphoreType.DMA
    scratch = [
        pltpu.VMEM((rows, width), bf),
        pltpu.VMEM(gate_weight.shape[1:], bf),
        pltpu.VMEM(up_weight.shape[1:], bf),
        pltpu.VMEM((2, hidden, half), bf),
        pltpu.VMEM((groups, *enc_weight.shape), bf),
        pltpu.VMEM((groups, *dec_weight.shape), bf),
        pltpu.VMEM((2, groups * rows, half), bf),
        pltpu.VMEM((rows, 128), bf),
        pltpu.VMEM((groups, rows, 128), bf),
        pltpu.VMEM((groups * rows, 128), f32),
        pltpu.VMEM((rows, half), f32),
        pltpu.VMEM((rows, dec_weight.shape[1]), f32),
        pltpu.VMEM((2, band * rows, hidden), bf),
        pltpu.VMEM((depth, band, 2, rows, half), bf),
        pltpu.VMEM((depth, LINES, 2, rows, half), bf),
        pltpu.VMEM((depth, LINES, rows, half), bf),
        pltpu.VMEM((depth, LINES, rows, half), bf),
        pltpu.VMEM((depth, LINES, rows, half), f32),
        pltpu.VMEM((depth, rows, half), bf),
        pltpu.VMEM((depth, rows, half), bf),
        pltpu.VMEM((depth, rows, half), bf),
        pltpu.VMEM((depth, rows, half), bf),
        pltpu.VMEM((2, rows, half), bf),
        *[dma((groups,)), dma((4 * depth + 1,))] * 4,
        dma((1,)), dma((1,)),
        dma((depth, LINES)), dma((depth, LINES)),
        dma((groups,)), dma((2 * depth,)), dma((groups,)), dma((2 * depth,)),
        dma((depth, LINES)), dma((depth, LINES)), dma((depth,)), dma((depth,)), dma((depth,)), dma((depth,)),
        dma((1,)), dma((1,)), dma((4,)),
    ]
    return pl.pallas_call(
        layer_kernel,
        out_shape=jax.ShapeDtypeStruct((rows, dec_weight.shape[1]), bf),
        in_specs=[anywhere, vmem, vmem, vmem, anywhere, anywhere, anywhere, vmem],
        out_specs=vmem,
        scratch_shapes=scratch,
        compiler_params=pltpu.CompilerParams(
            collective_id=0, has_side_effects=True, vmem_limit_bytes=60 * 1024 * 1024
        ),
    )(tokens, enc_weight, routes, gates, gate_weight, up_weight, down_weight, dec_weight)


def on_device(tokens, enc_weight, routes, *rest):
    token_count, choice_count = routes.shape
    plan = whole_layer if 2 * choice_count >= lax.axis_size("expert") else exchange_slots
    return plan(tokens, enc_weight, routes, *rest)


def solution(mesh):
    in_specs = (
        P("expert", None),
        P("expert", "hidden"),
        P("expert", None),
        P("expert", None),
        P("expert", None, "hidden"),
        P("expert", None, "hidden"),
        P("expert", None, "hidden"),
        P("expert", "hidden"),
    )
    out_specs = P("expert", "hidden")
    return jax.shard_map(
        on_device, mesh=mesh, in_specs=in_specs, out_specs=out_specs, check_vma=False
    )
```
